32 devices in a mesh: train: 8 (over z, core), query: 4 (over y, x).
Axes of the slice: x: 2, y: 2, z: 4, core: 2. Of those that a mesh axis runs over, the one named last changes fastest.
Arguments:
- train_losses: float32 [256, 65536], P('train', 'query'), may hold values from 0 to 16
- query_losses: float32 [256, 8192], P('train', 'query'), may hold values from 0 to 16
- chain_slots: int32 [32], replicated, may hold values from 0 to 31, as said below
- doc_lengths: int32 [64], replicated, may hold values from 1 to 4096, 65536 in all
Outputs:
- influence: float32 [64, 8192], P('train', 'query')
The draws below stay inside these ranges and needn't reach their ends.
Inputs may be any that keep to these rules, and one draw needn't show every extreme that they name: `chain_slots`: every chain appears exactly once. `doc_lengths`: the documents cover all 65536 train tokens in order.
All inputs are finite; a program needn't handle non-finite values.
Results may differ from the reference program's by a relative error of at most 0.00084.
Values may be sent and summed in bfloat16 or wider, within the bound.
A program may use at most 64 MiB of HBM per device.

```python
import math
import jax
import jax.numpy as jnp
import numpy as np
from jax import lax

DRAWS = 256
CHAINS = 32
DOC_LEN = 1024
NTRAIN = 65536
NQ = 8192
DOCS = 64


factor_count = 16


def shared_factors(key):
    return jax.random.normal(jax.random.fold_in(key, 11), (DRAWS, factor_count), jnp.float32)


def slot_order(key):
    return jax.random.permutation(jax.random.fold_in(key, 13), CHAINS).astype(jnp.int32)


def token_losses(key, factors, token_total, region_size):
    key_list = jax.random.split(key, 5)
    base_loss = jax.random.uniform(key_list[0], (token_total,), jnp.float32, 1.0, 8.0)
    spread = jnp.exp(jax.random.uniform(key_list[1], (token_total,), jnp.float32, jnp.log(0.05), jnp.log(1.0)))
    jitter = jax.random.normal(key_list[2], (DRAWS, token_total), jnp.float32)
    region_count = (token_total + region_size - 1) // region_size
    regions = jax.random.normal(key_list[3], (region_count, factor_count), jnp.float32)
    loadings = regions[jnp.arange(token_total) // region_size] + 0.5 * jax.random.normal(key_list[4], (token_total, factor_count), jnp.float32)
    signal = jnp.dot(factors, loadings.T) * 0.5
    return jnp.clip(base_loss[None, :] + spread[None, :] * (signal + jitter), 0.0, 16.0)


def draw_train_losses(key, part):
    slot_chain = slot_order(key)
    factors = shared_factors(key).reshape(CHAINS, DRAWS // CHAINS, factor_count)[slot_chain].reshape(DRAWS, factor_count)
    return token_losses(jax.random.fold_in(key, 21), factors, NTRAIN, DOC_LEN)


def draw_query_losses(key, part):
    return token_losses(jax.random.fold_in(key, 31), shared_factors(key), NQ, 64)


def draw_chain_slots(key, part):
    return slot_order(key)


def split_up(count, total, reach, slope):
    loads = [(1 << 20) // math.isqrt(grade ** slope) + 1 for grade in range(2, count + 1)]
    surplus, counts = total - reach - (count - 1), [1] * (count - 1)
    while surplus > 0:
        movable = [i for i in range(count - 1) if counts[i] < reach]
        pool, remaining = sum([loads[i] for i in movable]), surplus
        for i in movable:
            more = min(reach - counts[i], max(1, remaining * loads[i] // pool), surplus)
            counts[i] = counts[i] + more
            surplus = surplus - more
    return np.array([reach] + counts)


def ragged_sizes(rng, number_of, total, bound, slope):
    if number_of == 2:
        one = jax.random.randint(rng, (), max(1, total - bound), min(bound, total - 1) + 1)
        return jnp.stack([one, total - one])
    tallies = jnp.asarray(split_up(number_of, total, bound, slope), jnp.int32)
    couples = (number_of - 1) // 2
    source_of, receiver = tallies[1:1 + 2 * couples:2], tallies[2:2 + 2 * couples:2]
    margin = jnp.minimum(source_of - 1, bound - receiver)
    shifted = jax.random.randint(jax.random.fold_in(rng, 1), (couples,), 0, 1 << 20) % (margin + 1)
    tallies = tallies.at[1:1 + 2 * couples:2].set(source_of - shifted).at[2:2 + 2 * couples:2].set(receiver + shifted)
    return tallies[jax.random.permutation(jax.random.fold_in(rng, 2), number_of)]


def setup_inputs(seed: int = 0) -> dict:
    keys = jax.random.split(jax.random.key(seed), 5)
    train_losses = draw_train_losses(jax.random.fold_in(keys[4], 71), 0)
    query_losses = draw_query_losses(jax.random.fold_in(keys[4], 71), 0)
    chain_slots = draw_chain_slots(jax.random.fold_in(keys[4], 71), 0)
    doc_lengths = ragged_sizes(keys[3], DOCS, NTRAIN, 4 * DOC_LEN, 2).astype(jnp.int32)
    return dict(train_losses=train_losses, query_losses=query_losses, chain_slots=chain_slots, doc_lengths=doc_lengths)


def reference(train_losses, query_losses, chain_slots, doc_lengths):
    highest = lax.Precision.HIGHEST
    train_mean = lax.optimization_barrier(jnp.sum(train_losses, axis=0)) / DRAWS
    train_centered = (train_losses - train_mean[None, :]).astype(jnp.bfloat16)
    query_mean = lax.optimization_barrier(jnp.sum(query_losses, axis=0)) / DRAWS
    query_centered = (query_losses - query_mean[None, :]).astype(jnp.bfloat16)
    per_chain = DRAWS // CHAINS
    query_paired = jnp.take(query_centered.reshape(CHAINS, per_chain, NQ), chain_slots, axis=0).reshape(DRAWS, NQ)
    train_wide = train_centered.astype(jnp.float32)
    query_wide = query_paired.astype(jnp.float32)
    train_scale = lax.rsqrt(lax.optimization_barrier(jnp.sum(train_wide * train_wide, axis=0)) / (DRAWS - 1) + 1e-06)
    query_scale = lax.rsqrt(lax.optimization_barrier(jnp.sum(query_wide * query_wide, axis=0)) / (DRAWS - 1) + 1e-06)
    doc_ends = jnp.cumsum(doc_lengths).astype(jnp.int32)
    doc_starts = (doc_ends - doc_lengths).astype(jnp.int32)
    block_rows = math.gcd(NTRAIN, 4096)
    block_count = NTRAIN // block_rows

    def one_block(running, block_index):
        offset = (block_index * block_rows).astype(jnp.int32)
        portion = lax.dynamic_slice_in_dim(train_centered, offset, block_rows, 1)
        scales = lax.dynamic_slice_in_dim(train_scale, offset, block_rows, 0)
        covariance = lax.dot_general(portion, query_paired, (((0,), (0,)), ((), ())), preferred_element_type=jnp.float32)
        correlation = covariance * scales[:, None] * query_scale[None, :] / (DRAWS - 1)
        signed = correlation * jnp.abs(correlation)
        positions = offset + jnp.arange(block_rows, dtype=jnp.int32)
        inside = (positions[:, None] >= doc_starts[None, :]) & (positions[:, None] < doc_ends[None, :])
        member = inside.astype(jnp.float32)
        added = lax.dot_general(member, signed, (((0,), (0,)), ((), ())), precision=highest, preferred_element_type=jnp.float32)
        return (running + added, None)
    start_value = jnp.zeros((DOCS, NQ), jnp.float32)
    pooled, _ = lax.scan(one_block, start_value, jnp.arange(block_count, dtype=jnp.int32))
    return pooled / doc_lengths[:, None].astype(jnp.float32)
```

```python
import functools

import jax
import jax.numpy as jnp
from jax import lax
from jax.experimental import pallas as pl
from jax.experimental.pallas import tpu as pltpu
from jax.sharding import PartitionSpec as P

MESH = pl.DeviceIdType.MESH
epsilon = 1e-06
per_chain = 8


def remote(src, dst, send, recv, device):
    return pltpu.make_async_remote_copy(
        src_ref=src, dst_ref=dst, send_sem=send, recv_sem=recv, device_id=device, device_id_type=MESH
    )


def gather_kernel(
    n_t, n_q, x_ref, y_ref, g_ref, q_ref,
    sums, parts, means, cent, centq,
    s1, r1, s2, r2, sa, ra, sq, rq, sf, rf, sb, rb, sr, rr, s0, r0, sh, rh, local_sem,
):
    t = lax.axis_index("train")
    q = lax.axis_index("query")
    n_m, n_a = n_t // 2, n_q // 2
    m, c = t // 2, lax.rem(t, 2)
    sibling = 2 * m + 1 - c
    a, b = q // 2, lax.rem(q, 2)
    partner = 2 * a + 1 - b
    others = [lax.rem(a + k, n_a) for k in range(1, n_a)]
    columns = [2 * other + b for other in others]
    half = cent.shape[3]
    piece = 2 * half
    spread = y_ref.shape[1] // n_t
    draws = x_ref.shape[0] * n_t

    barrier = pltpu.get_barrier_semaphore()
    for k in range(1, n_t):
        pl.semaphore_signal(barrier, inc=1, device_id=(lax.rem(t + k, n_t), q), device_id_type=MESH)
    for target in [partner] + columns:
        pl.semaphore_signal(barrier, inc=1, device_id=(t, target), device_id_type=MESH)
    for r in range(n_t):
        sums[r, :, 0:piece] = jnp.sum(x_ref[:, r * piece:(r + 1) * piece], axis=0, keepdims=True)
        sums[r, :, piece:piece + spread] = jnp.sum(
            y_ref[:, r * spread:(r + 1) * spread], axis=0, keepdims=True
        )
    pl.semaphore_wait(barrier, n_t - 1 + n_a)

    sends, sources = [sibling], [sibling]
    for k in range(1, n_m):
        up, down = lax.rem(m + k, n_m), lax.rem(m + n_m - k, n_m)
        sends += [2 * up + c, 2 * up + 1 - c]
        sources += [2 * down + c, 2 * down + 1 - c]

    started = []
    for r in sends:
        copy = remote(sums.at[r], parts.at[t], s1.at[r], r1.at[t], (r, q))
        copy.start()
        started.append(copy)
    total = sums[t]
    for r in sources:
        remote(parts.at[r], parts.at[r], s1.at[r], r1.at[r], (r, q)).wait_recv()
        total = total + parts[r]
    means[t] = total / draws
    for r in sends:
        copy = remote(means.at[t], means.at[t], s2.at[r], r2.at[t], (r, q))
        copy.start()
        started.append(copy)

    def center(r):
        for h in range(2):
            begin = pl.multiple_of(r * piece + h * half, 128)
            cent[r, h] = (
                x_ref[:, pl.ds(begin, half)] - means[r, :, h * half:(h + 1) * half]
            ).astype(jnp.bfloat16)
        begin = pl.multiple_of(r * spread, 128)
        centq[:, pl.ds(begin, spread)] = (
            y_ref[:, pl.ds(begin, spread)] - means[r, :, piece:piece + spread]
        ).astype(jnp.bfloat16)

    def spread_block(src, tp):
        copy = remote(src, g_ref.at[q, :, tp], sb.at[tp], rb.at[tp], (t, partner))
        copy.start()
        started.append(copy)
        for k in range(n_a - 1):
            copy = remote(src, g_ref.at[q, :, tp], sr.at[tp, others[k]], rr.at[tp, a], (t, columns[k]))
            copy.start()
            started.append(copy)

    def pass_on(tp):
        whole = g_ref.at[partner, :, tp]
        remote(whole, whole, sb.at[tp], rb.at[tp], (t, partner)).wait_recv()
        for k in range(n_a - 1):
            first = g_ref.at[partner, 0, tp]
            copy = remote(first, first, s0.at[tp, others[k]], r0.at[tp, a], (t, columns[k]))
            copy.start()
            started.append(copy)
        for k in range(n_a - 1):
            whole = g_ref.at[columns[k], :, tp]
            remote(whole, whole, sr.at[tp, others[k]], rr.at[tp, others[k]], (t, columns[k])).wait_recv()
            second = g_ref.at[columns[k], 1, tp]
            copy = remote(second, second, sh.at[tp, others[k]], rh.at[tp, others[k]], (t, partner))
            copy.start()
            started.append(copy)

    center(t)
    spread_block(cent.at[t], t)
    own = pltpu.make_async_copy(cent.at[t], g_ref.at[q, :, t], local_sem.at[0])
    own.start()
    arrivals = [sibling]
    for k in range(1, n_m):
        down = lax.rem(m + n_m - k, n_m)
        arrivals += [2 * down + c, 2 * down + 1 - c]
    sent = [sends[i] for i in range(1, n_t - 1)] + [sends[0]]
    for r in sent:
        remote(means.at[r], means.at[r], s2.at[r], r2.at[r], (r, q)).wait_recv()
        center(r)
        copy = remote(cent.at[r], g_ref.at[q, :, t], sa.at[r], ra.at[t], (r, q))
        copy.start()
        started.append(copy)
    for k in range(1, n_m):
        up = lax.rem(m + k, n_m)
        copy = remote(centq, q_ref.at[t], sq.at[up], rq.at[m], (2 * up + c, q))
        copy.start()
        started.append(copy)
    copy = remote(centq, q_ref.at[t], sf.at[m], rf.at[m], (sibling, q))
    copy.start()
    started.append(copy)
    ownq = pltpu.make_async_copy(centq, q_ref.at[t], local_sem.at[1])
    ownq.start()

    before = t
    for tp in arrivals:
        block = g_ref.at[q, :, tp]
        remote(block, block, sa.at[tp], ra.at[tp], (tp, q)).wait_recv()
        spread_block(block, tp)
        pass_on(before)
        before = tp
    pass_on(before)
    for k in range(1, n_m):
        down = lax.rem(m + n_m - k, n_m)
        block = q_ref.at[2 * down + c]
        remote(block, block, sq.at[down], rq.at[down], (2 * down + c, q)).wait_recv()
        copy = remote(block, block, sf.at[down], rf.at[down], (sibling, q))
        copy.start()
        started.append(copy)
    for k in range(n_m):
        block = q_ref.at[2 * k + 1 - c]
        remote(block, block, sf.at[k], rf.at[k], (sibling, q)).wait_recv()
    for tp in [t] + arrivals:
        for k in range(n_a - 1):
            diagonal = 2 * others[k] + 1 - b
            first = g_ref.at[diagonal, 0, tp]
            remote(first, first, s0.at[tp, others[k]], r0.at[tp, others[k]], (t, columns[k])).wait_recv()
            second = g_ref.at[diagonal, 1, tp]
            remote(second, second, sh.at[tp, others[k]], rh.at[tp, others[k]], (t, partner)).wait_recv()
    for copy in started:
        copy.wait_send()
    own.wait()
    ownq.wait()


def gather(train_losses, query_losses, n_t, n_q):
    draws_here, tokens = train_losses.shape
    queries = query_losses.shape[1]
    half = tokens // n_t // 2
    width = 2 * half + queries // n_t
    n_m, n_a = n_t // 2, n_q // 2
    dma = pltpu.SemaphoreType.DMA
    bf16 = jnp.bfloat16
    return pl.pallas_call(
        functools.partial(gather_kernel, n_t, n_q),
        out_shape=(
            jax.ShapeDtypeStruct((n_q, 2, n_t, draws_here, half), bf16),
            jax.ShapeDtypeStruct((n_t, draws_here, queries), bf16),
        ),
        in_specs=[pl.BlockSpec(memory_space=pltpu.VMEM)] * 2,
        out_specs=[pl.BlockSpec(memory_space=pl.ANY)] * 2,
        scratch_shapes=[
            pltpu.VMEM((n_t, 1, width), jnp.float32),
            pltpu.VMEM((n_t, 1, width), jnp.float32),
            pltpu.VMEM((n_t, 1, width), jnp.float32),
            pltpu.VMEM((n_t, 2, draws_here, half), bf16),
            pltpu.VMEM((draws_here, queries), bf16),
            dma((n_t,)), dma((n_t,)), dma((n_t,)), dma((n_t,)), dma((n_t,)), dma((n_t,)),
            dma((n_m,)), dma((n_m,)), dma((n_m,)), dma((n_m,)),
            dma((n_t,)), dma((n_t,)),
            dma((n_t, n_a)), dma((n_t, n_a)), dma((n_t, n_a)), dma((n_t, n_a)),
            dma((n_t, n_a)), dma((n_t, n_a)),
            dma((2,)),
        ],
        compiler_params=pltpu.CompilerParams(
            collective_id=0, has_side_effects=True, vmem_limit_bytes=40 << 20
        ),
    )(train_losses, query_losses)


def pool_kernel(
    lengths, slots, rank, g_ref, q_ref, out_ref, wide, paired, acc, turned, weights, ends, *, tokens, piece
):
    step = pl.program_id(0)
    draws, half = g_ref.shape[1], g_ref.shape[2]
    docs, queries = out_ref.shape
    tile = min(256, half)
    strip = min(256, queries)

    @pl.when(step == 0)
    def _():
        wide[...] = q_ref[...].astype(jnp.float32)

        def pair(s, carry):
            first = pl.multiple_of(slots[2 * s] * per_chain, per_chain)
            second = pl.multiple_of(slots[2 * s + 1] * per_chain, per_chain)
            rows = jnp.concatenate(
                [wide[pl.ds(first, per_chain), :], wide[pl.ds(second, per_chain), :]], axis=0
            )
            target = pl.multiple_of(s * 2 * per_chain, 2 * per_chain)
            paired[pl.ds(target, 2 * per_chain), :] = rows.astype(jnp.bfloat16)
            return carry

        lax.fori_loop(0, draws // per_chain // 2, pair, 0)

        def end(k, total):
            total = total + lengths[k]
            ends[k] = total
            return total

        lax.fori_loop(0, docs, end, jnp.int32(0))

        def clear(k, carry):
            acc[k] = jnp.zeros(acc.shape[1:], jnp.float32)
            return carry

        lax.fori_loop(0, docs, clear, 0)

    block = g_ref[0]
    widened = block.astype(jnp.float32)
    squares = jnp.sum(widened * widened, axis=0, keepdims=True)
    weight = 1.0 / (squares / (draws - 1) + epsilon)
    weights[...] = jnp.transpose(jnp.broadcast_to(weight, (128, half)))
    turned[...] = jnp.transpose(block)

    base = (step // 2) * tokens + rank[0] * piece + lax.rem(step, 2) * half

    first_doc = lax.while_loop(lambda k: ends[k] <= base, lambda k: k + 1, jnp.int32(0))

    def body(state):
        at, doc = state
        row = pl.multiple_of(at // tile * tile, tile)
        stop = jnp.minimum(row + tile, ends[doc] - base)
        places = row + lax.broadcasted_iota(jnp.int32, (tile, 128), 0)
        inside = (places >= at) & (places < stop)
        wt = jnp.where(inside, weights[pl.ds(row, tile), :], 0.0)
        wt = jnp.concatenate([wt] * (strip // 128), axis=1)
        lhs = turned[pl.ds(row, tile), :]
        for n in range(queries // strip):
            cov = jnp.dot(
                lhs, paired[:, n * strip:(n + 1) * strip], preferred_element_type=jnp.float32
            )
            signed = cov * jnp.abs(cov) * wt
            part = jnp.sum(signed.reshape(tile // 8, 8, strip), axis=0)
            acc[doc, :, n * strip:(n + 1) * strip] += part
        return stop, jnp.where(stop >= ends[doc] - base, doc + 1, doc)

    lax.while_loop(lambda state: state[0] < half, body, (jnp.int32(0), first_doc))

    @pl.when(step == pl.num_programs(0) - 1)
    def _():
        chosen = paired[...].astype(jnp.float32)
        squares = jnp.sum(chosen * chosen, axis=0, keepdims=True)
        scale = 1.0 / (squares / (draws - 1) + epsilon) / ((draws - 1) * (draws - 1))

        def finish(k, carry):
            pooled = jnp.sum(acc[k], axis=0, keepdims=True)
            out_ref[pl.ds(k, 1), :] = pooled * scale / lengths[k].astype(jnp.float32)
            return carry

        lax.fori_loop(0, docs, finish, 0)


def pool(lengths, slots, rank, pieces, query, tokens, piece):
    chunks, draws, half = pieces.shape
    queries = query.shape[1]
    docs = lengths.shape[0]
    return pl.pallas_call(
        functools.partial(pool_kernel, tokens=tokens, piece=piece),
        out_shape=jax.ShapeDtypeStruct((docs, queries), jnp.float32),
        grid_spec=pltpu.PrefetchScalarGridSpec(
            num_scalar_prefetch=3,
            grid=(chunks,),
            in_specs=[
                pl.BlockSpec((1, draws, half), lambda i, *_: (i, 0, 0)),
                pl.BlockSpec((draws, queries), lambda i, *_: (0, 0)),
            ],
            out_specs=pl.BlockSpec((docs, queries), lambda i, *_: (0, 0)),
            scratch_shapes=[
                pltpu.VMEM((draws, queries), jnp.float32),
                pltpu.VMEM((draws, queries), jnp.bfloat16),
                pltpu.VMEM((docs, 8, queries), jnp.float32),
                pltpu.VMEM((half, draws), jnp.bfloat16),
                pltpu.VMEM((half, 128), jnp.float32),
                pltpu.SMEM((docs,), jnp.int32),
            ],
        ),
        compiler_params=pltpu.CompilerParams(
            dimension_semantics=("arbitrary",), vmem_limit_bytes=48 << 20
        ),
    )(lengths, slots, rank, pieces, query)


def scatter_kernel(n_t, p_ref, out_ref, near, total, far, s1, r1, s2, r2):
    t = lax.axis_index("train")
    q = lax.axis_index("query")
    n_m = n_t // 2
    m, c = t // 2, lax.rem(t, 2)
    sibling = 2 * m + 1 - c
    barrier = pltpu.get_barrier_semaphore()
    pl.semaphore_signal(barrier, inc=1, device_id=(sibling, q), device_id_type=MESH)
    for k in range(1, n_m):
        other = 2 * lax.rem(m + k, n_m) + c
        pl.semaphore_signal(barrier, inc=1, device_id=(other, q), device_id_type=MESH)
    pl.semaphore_wait(barrier, n_m)
    started = []
    chips = [lax.rem(m + k, n_m) for k in range(1, n_m)] + [m]
    for chip in chips:
        copy = remote(p_ref.at[chip, 1 - c], near.at[chip], s1.at[chip], r1.at[chip], (sibling, q))
        copy.start()
        started.append(copy)
    for chip in chips:
        remote(near.at[chip], near.at[chip], s1.at[chip], r1.at[chip], (sibling, q)).wait_recv()
        total[chip] = p_ref[chip, c] + near[chip]
        if chip is not m:
            copy = remote(total.at[chip], far.at[m], s2.at[chip], r2.at[m], (2 * chip + c, q))
            copy.start()
            started.append(copy)
    result = total[m]
    for k in range(1, n_m):
        chip = lax.rem(m + n_m - k, n_m)
        remote(far.at[chip], far.at[chip], s2.at[chip], r2.at[chip], (2 * chip + c, q)).wait_recv()
        result = result + far[chip]
    out_ref[...] = result
    for copy in started:
        copy.wait_send()


def scatter(partial, n_t):
    docs, queries = partial.shape
    here = docs // n_t
    n_m = n_t // 2
    dma = pltpu.SemaphoreType.DMA
    block = pltpu.VMEM((n_m, here, queries), jnp.float32)
    return pl.pallas_call(
        functools.partial(scatter_kernel, n_t),
        out_shape=jax.ShapeDtypeStruct((here, queries), jnp.float32),
        in_specs=[pl.BlockSpec(memory_space=pltpu.VMEM)],
        out_specs=pl.BlockSpec(memory_space=pltpu.VMEM),
        scratch_shapes=[block, block, block, dma((n_m,)), dma((n_m,)), dma((n_m,)), dma((n_m,))],
        compiler_params=pltpu.CompilerParams(
            collective_id=1, has_side_effects=True, vmem_limit_bytes=16 << 20
        ),
    )(partial.reshape(n_m, 2, here, queries))


def shards(train_losses, query_losses, chain_slots, doc_lengths):
    n_t = lax.axis_size("train")
    n_q = lax.axis_size("query")
    draws_here, tokens = train_losses.shape
    queries = query_losses.shape[1]
    draws = draws_here * n_t
    piece = tokens // n_t
    pieces, query = gather(train_losses, query_losses, n_t, n_q)
    rank = lax.axis_index("train").astype(jnp.int32).reshape(1)
    partial = pool(
        doc_lengths, chain_slots, rank,
        pieces.reshape(n_q * 2, draws, piece // 2), query.reshape(draws, queries), tokens, piece,
    )
    return scatter(partial, n_t)


def solution(mesh):
    in_specs = (P("train", "query"), P("train", "query"), P(), P())
    out_specs = P("train", "query")
    return jax.shard_map(shards, mesh=mesh, in_specs=in_specs, out_specs=out_specs, check_vma=False)
```

```python
import functools

import jax
import jax.numpy as jnp
from jax import lax
from jax.experimental import pallas as pl
from jax.experimental.pallas import tpu as pltpu
from jax.sharding import PartitionSpec as P

MESH = pl.DeviceIdType.MESH
epsilon = 1e-06
per_chain = 8


def remote(src, dst, send, recv, device):
    return pltpu.make_async_remote_copy(
        src_ref=src, dst_ref=dst, send_sem=send, recv_sem=recv, device_id=device, device_id_type=MESH
    )


chunks = 4


def fused_kernel(
    n_t, n_q, x_ref, y_ref, slots_ref, lengths_ref, out_ref,
    sums, parts, means, cent, centq, held, whole_q, turned, scales, acc,
    s1, r1, s2, r2, sa, ra, sq, rq, sf, rf, sb, rb, sr, rr, s0, r0, sh, rh, local_sem,
):
    t = lax.axis_index("train")
    q = lax.axis_index("query")
    n_m, n_a = n_t // 2, n_q // 2
    m, c = t // 2, lax.rem(t, 2)
    sibling = 2 * m + 1 - c
    a, b = q // 2, lax.rem(q, 2)
    partner = 2 * a + 1 - b
    others = [lax.rem(a + k, n_a) for k in range(1, n_a)]
    columns = [2 * other + b for other in others]
    diagonals = [2 * other + 1 - b for other in others]
    size = cent.shape[3]
    half = size // 2
    piece = chunks * size
    queries = y_ref.shape[1]
    spread = queries // n_t
    draws = x_ref.shape[0] * n_t
    tokens = x_ref.shape[1]
    docs = out_ref.shape[0]

    barrier = pltpu.get_barrier_semaphore()
    for k in range(1, n_t):
        pl.semaphore_signal(barrier, inc=1, device_id=(lax.rem(t + k, n_t), q), device_id_type=MESH)
    for target in [partner] + columns:
        pl.semaphore_signal(barrier, inc=1, device_id=(t, target), device_id_type=MESH)
    for r in range(n_t):
        sums[r, :, 0:piece] = jnp.sum(x_ref[:, r * piece:(r + 1) * piece], axis=0, keepdims=True)
        sums[r, :, piece:piece + spread] = jnp.sum(
            y_ref[:, r * spread:(r + 1) * spread], axis=0, keepdims=True
        )
    pl.semaphore_wait(barrier, n_t - 1 + n_a)

    sends, sources = [sibling], [sibling]
    for k in range(1, n_m):
        up, down = lax.rem(m + k, n_m), lax.rem(m + n_m - k, n_m)
        sends += [2 * up + c, 2 * up + 1 - c]
        sources += [2 * down + c, 2 * down + 1 - c]

    started = []
    for r in sends:
        copy = remote(sums.at[r], parts.at[t], s1.at[r], r1.at[t], (r, q))
        copy.start()
        started.append(copy)
    total = sums[t]
    for r in sources:
        remote(parts.at[r], parts.at[r], s1.at[r], r1.at[r], (r, q)).wait_recv()
        total = total + parts[r]
    means[t] = total / draws
    for r in sends:
        copy = remote(means.at[t], means.at[t], s2.at[r], r2.at[t], (r, q))
        copy.start()
        started.append(copy)

    def center(r, j):
        begin = pl.multiple_of(r * piece + j * size, 128)
        mean = means[r, :, j * size:(j + 1) * size]
        cent[r, j] = (x_ref[:, pl.ds(begin, size)] - mean).astype(jnp.bfloat16)

    def center_query(r):
        begin = pl.multiple_of(r * spread, 128)
        centq[:, pl.ds(begin, spread)] = (
            y_ref[:, pl.ds(begin, spread)] - means[r, :, piece:piece + spread]
        ).astype(jnp.bfloat16)

    def spread_block(src, j, tp):
        remote(src, held.at[q, j, tp], sb.at[j], rb.at[j, tp], (t, partner)).start()
        for k in range(n_a - 1):
            remote(
                src, held.at[q, j, tp], sr.at[j, others[k]], rr.at[j, tp, a], (t, columns[k])
            ).start()

    def pass_on(j, tp):
        block = held.at[partner, j, tp]
        remote(block, block, sb.at[j], rb.at[j, tp], (t, partner)).wait_recv()
        first = held.at[partner, j, tp, :, pl.ds(0, half)]
        for k in range(n_a - 1):
            remote(first, first, s0.at[j, others[k]], r0.at[j, a], (t, columns[k])).start()
        for k in range(n_a - 1):
            block = held.at[columns[k], j, tp]
            remote(
                block, block, sr.at[j, others[k]], rr.at[j, tp, others[k]], (t, columns[k])
            ).wait_recv()
            second = held.at[columns[k], j, tp, :, pl.ds(half, half)]
            remote(second, second, sh.at[j, others[k]], rh.at[j, others[k]], (t, partner)).start()

    locals_ = []
    for j in range(chunks):
        center(t, j)
        copy = pltpu.make_async_copy(cent.at[t, j], held.at[q, j, t], local_sem.at[j])
        copy.start()
        locals_.append(copy)
    center_query(t)
    for j in range(chunks):
        for r in sends:
            if j == 0:
                remote(means.at[r], means.at[r], s2.at[r], r2.at[r], (r, q)).wait_recv()
            center(r, j)
            remote(cent.at[r, j], held.at[q, j, t], sa.at[j], ra.at[j, t], (r, q)).start()
        if j == 0:
            spread_block(cent.at[t, 0], 0, t)
            for r in sends:
                center_query(r)
            for k in range(1, n_m):
                up = lax.rem(m + k, n_m)
                copy = remote(centq, whole_q.at[t], sq.at[up], rq.at[m], (2 * up + c, q))
                copy.start()
                started.append(copy)
            copy = remote(centq, whole_q.at[t], sf.at[m], rf.at[m], (sibling, q))
            copy.start()
            started.append(copy)
            ownq = pltpu.make_async_copy(centq, whole_q.at[t], local_sem.at[chunks])
            ownq.start()
            locals_.append(ownq)

    def stage(j, units, first=False):
        if not first:
            spread_block(cent.at[t, j], j, t)
        before = t
        due = 0
        for i, tp in enumerate(sources):
            block = held.at[q, j, tp]
            remote(block, block, sa.at[j], ra.at[j, tp], (tp, q)).wait_recv()
            spread_block(block, j, tp)
            pass_on(j, before)
            before = tp
            while due < len(units) and due * (n_t - 1) <= i * len(units):
                units[due]()
                due += 1
        pass_on(j, before)
        for unit in units[due:]:
            unit()

    def settle(j):
        for k in range(n_a - 1):
            first = held.at[diagonals[k], j, :, :, pl.ds(0, half)]
            remote(first, first, s0.at[j, others[k]], r0.at[j, others[k]], (t, columns[k])).wait_recv()
            second = held.at[diagonals[k], j, :, :, pl.ds(half, half)]
            remote(second, second, sh.at[j, others[k]], rh.at[j, others[k]], (t, partner)).wait_recv()

    wide = jnp.broadcast_to(lengths_ref[...].astype(jnp.float32), (docs, docs))
    row = lax.broadcasted_iota(jnp.int32, (docs, docs), 0)
    column = lax.broadcasted_iota(jnp.int32, (docs, docs), 1)
    doc_ends = jnp.sum(jnp.where(column <= row, wide, 0.0), axis=1, keepdims=True)
    doc_starts = jnp.sum(jnp.where(column < row, wide, 0.0), axis=1, keepdims=True)
    strip = min(256, queries)

    def unit(col, j):
        block = held[col, j].reshape(draws, size)
        widened = block.astype(jnp.float32)
        squares = jnp.sum(widened * widened, axis=0, keepdims=True)
        weight = 1.0 / (squares / (draws - 1) + epsilon)
        high = weight.astype(jnp.bfloat16).astype(jnp.float32)
        low = weight - high
        base = col * tokens + t * piece + j * size
        places = (base + lax.broadcasted_iota(jnp.int32, (docs, size), 1)).astype(jnp.float32)
        inside = (places >= doc_starts) & (places < doc_ends)
        member = jnp.concatenate(
            [jnp.where(inside, high, 0.0), jnp.where(inside, low, 0.0)], axis=0
        ).astype(jnp.bfloat16)

        def add_strip(n, carry):
            begin = pl.multiple_of(n * strip, strip)
            cov = jnp.dot(
                turned[pl.ds(begin, strip), :], block, preferred_element_type=jnp.float32
            )
            signed = cov * jnp.abs(cov)
            top = signed.astype(jnp.bfloat16)
            rest = (signed - top.astype(jnp.float32)).astype(jnp.bfloat16)
            dims = (((1,), (1,)), ((), ()))
            pooled = lax.dot_general(top, member, dims, preferred_element_type=jnp.float32)
            pooled += lax.dot_general(rest, member, dims, preferred_element_type=jnp.float32)
            acc[pl.ds(begin, strip), :] += pooled
            return carry

        lax.fori_loop(0, queries // strip, add_strip, 0)

    order = [q, partner] + columns + diagonals

    acc[...] = jnp.zeros_like(acc)
    stage(0, [], first=True)
    for k in range(1, n_m):
        down = lax.rem(m + n_m - k, n_m)
        block = whole_q.at[2 * down + c]
        remote(block, block, sq.at[down], rq.at[down], (2 * down + c, q)).wait_recv()
        copy = remote(block, block, sf.at[down], rf.at[down], (sibling, q))
        copy.start()
        started.append(copy)
    for k in range(n_m):
        block = whole_q.at[2 * k + 1 - c]
        remote(block, block, sf.at[k], rf.at[k], (sibling, q)).wait_recv()
    for copy in locals_:
        copy.wait()

    slots = jnp.broadcast_to(slots_ref[...].astype(jnp.float32), (draws, draws // per_chain))
    row = lax.broadcasted_iota(jnp.int32, slots.shape, 0)
    slot = lax.broadcasted_iota(jnp.int32, slots.shape, 1)
    offset = row - slot * per_chain
    chosen = jnp.where(
        (offset >= 0) & (offset < per_chain), slots * per_chain + offset.astype(jnp.float32), 0.0
    )
    source = jnp.sum(chosen, axis=1, keepdims=True)
    place = lax.broadcasted_iota(jnp.int32, (draws, draws), 1).astype(jnp.float32)
    moves = jnp.where(place == source, 1.0, 0.0).astype(jnp.bfloat16)
    everything = whole_q[...].reshape(draws, queries)
    for n in range(queries // strip):
        part = jnp.dot(
            moves, everything[:, n * strip:(n + 1) * strip], preferred_element_type=jnp.float32
        )
        squares = jnp.sum(part * part, axis=0, keepdims=True)
        scales[:, n * strip:(n + 1) * strip] = (
            1.0 / (squares / (draws - 1) + epsilon) / ((draws - 1) * (draws - 1))
        )
        turned[n * strip:(n + 1) * strip, :] = jnp.transpose(part).astype(jnp.bfloat16)

    def step(j, carry):
        units = [functools.partial(unit, col, j - 1) for col in order]
        units[n_a + 1] = lambda: (settle(j - 1), unit(order[n_a + 1], j - 1))
        stage(j, units)
        return carry

    lax.fori_loop(1, chunks, step, 0)

    def last(i, carry):
        col = jnp.int32(0)
        for k in range(n_q):
            col = jnp.where(i == k, order[k], col)
        unit(col, chunks - 1)
        return carry

    lax.fori_loop(0, n_a + 1, last, 0)
    settle(chunks - 1)
    lax.fori_loop(n_a + 1, n_q, last, 0)

    for n in range(queries // strip):
        flat = jnp.transpose(acc[n * strip:(n + 1) * strip, :])
        out_ref[:, n * strip:(n + 1) * strip] = (
            (flat[0:docs] + flat[docs:2 * docs])
            * scales[:, n * strip:(n + 1) * strip]
            / (doc_ends - doc_starts)
        )

    for copy in started:
        copy.wait_send()
    for j in range(chunks):
        sent = cent.at[pl.ds(0, n_t - 1), j]
        remote(sent, sent, sa.at[j], ra.at[j, 0], (sibling, q)).wait_send()
        full = held.at[q, j]
        remote(full, full, sb.at[j], rb.at[j, 0], (t, partner)).wait_send()
        for k in range(n_a - 1):
            remote(full, full, sr.at[j, others[k]], rr.at[j, 0, 0], (t, partner)).wait_send()
            first = held.at[q, j, :, :, pl.ds(0, half)]
            remote(first, first, s0.at[j, others[k]], r0.at[j, 0], (t, partner)).wait_send()
            remote(first, first, sh.at[j, others[k]], rh.at[j, 0], (t, partner)).wait_send()


def fused(train_losses, query_losses, chain_slots, doc_lengths, n_t, n_q):
    draws_here, tokens = train_losses.shape
    queries = query_losses.shape[1]
    docs = doc_lengths.shape[0]
    draws = draws_here * n_t
    size = tokens // n_t // chunks
    width = chunks * size + queries // n_t
    n_m, n_a = n_t // 2, n_q // 2
    dma = pltpu.SemaphoreType.DMA
    bf16 = jnp.bfloat16
    vmem = pl.BlockSpec(memory_space=pltpu.VMEM)
    return pl.pallas_call(
        functools.partial(fused_kernel, n_t, n_q),
        out_shape=jax.ShapeDtypeStruct((docs, queries), jnp.float32),
        in_specs=[vmem] * 4,
        out_specs=vmem,
        scratch_shapes=[
            pltpu.VMEM((n_t, 1, width), jnp.float32),
            pltpu.VMEM((n_t, 1, width), jnp.float32),
            pltpu.VMEM((n_t, 1, width), jnp.float32),
            pltpu.VMEM((n_t, chunks, draws_here, size), bf16),
            pltpu.VMEM((draws_here, queries), bf16),
            pltpu.VMEM((n_q, chunks, n_t, draws_here, size), bf16),
            pltpu.VMEM((n_t, draws_here, queries), bf16),
            pltpu.VMEM((queries, draws), bf16),
            pltpu.VMEM((1, queries), jnp.float32),
            pltpu.VMEM((queries, 2 * docs), jnp.float32),
            dma((n_t,)), dma((n_t,)), dma((n_t,)), dma((n_t,)),
            dma((chunks,)), dma((chunks, n_t)),
            dma((n_m,)), dma((n_m,)), dma((n_m,)), dma((n_m,)),
            dma((chunks,)), dma((chunks, n_t)),
            dma((chunks, n_a)), dma((chunks, n_t, n_a)),
            dma((chunks, n_a)), dma((chunks, n_a)),
            dma((chunks, n_a)), dma((chunks, n_a)),
            dma((chunks + 1,)),
        ],
        compiler_params=pltpu.CompilerParams(
            collective_id=0, has_side_effects=True, vmem_limit_bytes=48 << 20
        ),
    )(train_losses, query_losses, chain_slots.reshape(1, -1), doc_lengths.reshape(1, -1))


def scatter_kernel(n_t, p_ref, out_ref, near, total, far, s1, r1, s2, r2):
    t = lax.axis_index("train")
    q = lax.axis_index("query")
    n_m = n_t // 2
    m, c = t // 2, lax.rem(t, 2)
    sibling = 2 * m + 1 - c
    barrier = pltpu.get_barrier_semaphore()
    pl.semaphore_signal(barrier, inc=1, device_id=(sibling, q), device_id_type=MESH)
    for k in range(1, n_m):
        other = 2 * lax.rem(m + k, n_m) + c
        pl.semaphore_signal(barrier, inc=1, device_id=(other, q), device_id_type=MESH)
    pl.semaphore_wait(barrier, n_m)
    started = []
    chips = [lax.rem(m + k, n_m) for k in range(1, n_m)] + [m]
    for chip in chips:
        copy = remote(p_ref.at[chip, 1 - c], near.at[chip], s1.at[chip], r1.at[chip], (sibling, q))
        copy.start()
        started.append(copy)
    for chip in chips:
        remote(near.at[chip], near.at[chip], s1.at[chip], r1.at[chip], (sibling, q)).wait_recv()
        total[chip] = p_ref[chip, c] + near[chip]
        if chip is not m:
            copy = remote(total.at[chip], far.at[m], s2.at[chip], r2.at[m], (2 * chip + c, q))
            copy.start()
            started.append(copy)
    result = total[m]
    for k in range(1, n_m):
        chip = lax.rem(m + n_m - k, n_m)
        remote(far.at[chip], far.at[chip], s2.at[chip], r2.at[chip], (2 * chip + c, q)).wait_recv()
        result = result + far[chip]
    out_ref[...] = result
    for copy in started:
        copy.wait_send()


def scatter(partial, n_t):
    docs, queries = partial.shape
    here = docs // n_t
    n_m = n_t // 2
    dma = pltpu.SemaphoreType.DMA
    block = pltpu.VMEM((n_m, here, queries), jnp.float32)
    return pl.pallas_call(
        functools.partial(scatter_kernel, n_t),
        out_shape=jax.ShapeDtypeStruct((here, queries), jnp.float32),
        in_specs=[pl.BlockSpec(memory_space=pltpu.VMEM)],
        out_specs=pl.BlockSpec(memory_space=pltpu.VMEM),
        scratch_shapes=[block, block, block, dma((n_m,)), dma((n_m,)), dma((n_m,)), dma((n_m,))],
        compiler_params=pltpu.CompilerParams(
            collective_id=1, has_side_effects=True, vmem_limit_bytes=16 << 20
        ),
    )(partial.reshape(n_m, 2, here, queries))


def shards(train_losses, query_losses, chain_slots, doc_lengths):
    n_t = lax.axis_size("train")
    n_q = lax.axis_size("query")
    partial = fused(train_losses, query_losses, chain_slots, doc_lengths, n_t, n_q)
    return scatter(partial, n_t)


def solution(mesh):
    in_specs = (P("train", "query"), P("train", "query"), P(), P())
    out_specs = P("train", "query")
    return jax.shard_map(shards, mesh=mesh, in_specs=in_specs, out_specs=out_specs, check_vma=False)
```

```python
import functools

import jax
import jax.numpy as jnp
from jax import lax
from jax.experimental import pallas as pl
from jax.experimental.pallas import tpu as pltpu
from jax.sharding import PartitionSpec as P

MESH = pl.DeviceIdType.MESH
epsilon = 1e-06
per_chain = 8


def remote(src, dst, send, recv, device):
    return pltpu.make_async_remote_copy(
        src_ref=src, dst_ref=dst, send_sem=send, recv_sem=recv, device_id=device, device_id_type=MESH
    )


chunks = 2
delay = 4


def fused_kernel(
    n_t, n_q, x_ref, y_ref, slots_ref, lengths_ref, out_ref,
    sums, parts, means, cent, centq, held, whole_q, turned, scales, acc,
    s1, r1, s2, r2, sa, ra, sq, rq, sf, rf, sb, rb, sr, rr, s0, r0, sh, rh, local_sem,
):
    t = lax.axis_index("train")
    q = lax.axis_index("query")
    n_m, n_a = n_t // 2, n_q // 2
    m, c = t // 2, lax.rem(t, 2)
    sibling = 2 * m + 1 - c
    a, b = q // 2, lax.rem(q, 2)
    partner = 2 * a + 1 - b
    others = [lax.rem(a + k, n_a) for k in range(1, n_a)]
    columns = [2 * other + b for other in others]
    diagonals = [2 * other + 1 - b for other in others]
    size = cent.shape[3]
    half = size // 2
    piece = chunks * size
    queries = y_ref.shape[1]
    spread = queries // n_t
    draws = x_ref.shape[0] * n_t
    tokens = x_ref.shape[1]
    docs = out_ref.shape[0]

    barrier = pltpu.get_barrier_semaphore()
    for k in range(1, n_t):
        pl.semaphore_signal(barrier, inc=1, device_id=(lax.rem(t + k, n_t), q), device_id_type=MESH)
    for target in [partner] + columns:
        pl.semaphore_signal(barrier, inc=1, device_id=(t, target), device_id_type=MESH)
    for r in range(n_t):
        sums[r, :, 0:piece] = jnp.sum(x_ref[:, r * piece:(r + 1) * piece], axis=0, keepdims=True)
        sums[r, :, piece:piece + spread] = jnp.sum(
            y_ref[:, r * spread:(r + 1) * spread], axis=0, keepdims=True
        )
    pl.semaphore_wait(barrier, n_t - 1 + n_a)

    sends, sources = [sibling], [sibling]
    for k in range(1, n_m):
        up, down = lax.rem(m + k, n_m), lax.rem(m + n_m - k, n_m)
        sends += [2 * up + c, 2 * up + 1 - c]
        sources += [2 * down + c, 2 * down + 1 - c]

    started = []
    for r in sends:
        copy = remote(sums.at[r], parts.at[t], s1.at[r], r1.at[t], (r, q))
        copy.start()
        started.append(copy)
    total = sums[t]
    for r in sources:
        remote(parts.at[r], parts.at[r], s1.at[r], r1.at[r], (r, q)).wait_recv()
        total = total + parts[r]
    means[t] = total / draws
    for r in sends:
        copy = remote(means.at[t], means.at[t], s2.at[r], r2.at[t], (r, q))
        copy.start()
        started.append(copy)

    def center(r, j):
        begin = pl.multiple_of(r * piece + j * size, 128)
        mean = means[r, :, j * size:(j + 1) * size]
        cent[r, j] = (x_ref[:, pl.ds(begin, size)] - mean).astype(jnp.bfloat16)

    def center_query(r):
        begin = pl.multiple_of(r * spread, 128)
        centq[:, pl.ds(begin, spread)] = (
            y_ref[:, pl.ds(begin, spread)] - means[r, :, piece:piece + spread]
        ).astype(jnp.bfloat16)

    def spread_block(src, j, tp):
        remote(src, held.at[q, j, tp], sb.at[j], rb.at[j, tp], (t, partner)).start()
        for k in range(n_a - 1):
            remote(
                src, held.at[q, j, tp], sr.at[j, others[k]], rr.at[j, tp, a], (t, columns[k])
            ).start()

    def pass_on(j, tp):
        block = held.at[partner, j, tp]
        remote(block, block, sb.at[j], rb.at[j, tp], (t, partner)).wait_recv()
        first = held.at[partner, j, tp, :, pl.ds(0, half)]
        for k in range(n_a - 1):
            remote(first, first, s0.at[j, others[k]], r0.at[j, a], (t, columns[k])).start()
        for k in range(n_a - 1):
            block = held.at[columns[k], j, tp]
            remote(
                block, block, sr.at[j, others[k]], rr.at[j, tp, others[k]], (t, columns[k])
            ).wait_recv()
            second = held.at[columns[k], j, tp, :, pl.ds(half, half)]
            remote(second, second, sh.at[j, others[k]], rh.at[j, others[k]], (t, partner)).start()

    locals_ = []
    for j in range(chunks):
        center(t, j)
        copy = pltpu.make_async_copy(cent.at[t, j], held.at[q, j, t], local_sem.at[j])
        copy.start()
        locals_.append(copy)
    center_query(t)
    for j in range(chunks):
        for r in sends:
            if j == 0:
                remote(means.at[r], means.at[r], s2.at[r], r2.at[r], (r, q)).wait_recv()
            center(r, j)
            remote(cent.at[r, j], held.at[q, j, t], sa.at[j], ra.at[j, t], (r, q)).start()
        if j == 0:
            spread_block(cent.at[t, 0], 0, t)
            for r in sends:
                center_query(r)
            for k in range(1, n_m):
                up = lax.rem(m + k, n_m)
                copy = remote(centq, whole_q.at[t], sq.at[up], rq.at[m], (2 * up + c, q))
                copy.start()
                started.append(copy)
            copy = remote(centq, whole_q.at[t], sf.at[m], rf.at[m], (sibling, q))
            copy.start()
            started.append(copy)
            ownq = pltpu.make_async_copy(centq, whole_q.at[t], local_sem.at[chunks])
            ownq.start()
            locals_.append(ownq)

    ranks = [t] + sources
    lag = min(delay, n_t - 1)

    def stage(j, units, first=False):
        due = 0
        for i, tp in enumerate(ranks):
            if i == 0:
                if not first:
                    spread_block(cent.at[t, j], j, t)
            else:
                block = held.at[q, j, tp]
                remote(block, block, sa.at[j], ra.at[j, tp], (tp, q)).wait_recv()
                spread_block(block, j, tp)
            if i >= lag:
                pass_on(j, ranks[i - lag])
            elif not first:
                pass_on(j - 1, ranks[n_t - lag + i])
            while due < len(units) and lag + due * (n_t - lag) // len(units) <= i + 1:
                units[due]()
                due += 1
        for unit in units[due:]:
            unit()

    def settle(j):
        for k in range(n_a - 1):
            first = held.at[diagonals[k], j, :, :, pl.ds(0, half)]
            remote(first, first, s0.at[j, others[k]], r0.at[j, others[k]], (t, columns[k])).wait_recv()
            second = held.at[diagonals[k], j, :, :, pl.ds(half, half)]
            remote(second, second, sh.at[j, others[k]], rh.at[j, others[k]], (t, partner)).wait_recv()

    wide = jnp.broadcast_to(lengths_ref[...].astype(jnp.float32), (docs, docs))
    row = lax.broadcasted_iota(jnp.int32, (docs, docs), 0)
    column = lax.broadcasted_iota(jnp.int32, (docs, docs), 1)
    doc_ends = jnp.sum(jnp.where(column <= row, wide, 0.0), axis=1, keepdims=True)
    doc_starts = jnp.sum(jnp.where(column < row, wide, 0.0), axis=1, keepdims=True)
    strip = min(512, queries)

    def unit(col, j):
        block = held[col, j].reshape(draws, size)
        widened = block.astype(jnp.float32)
        squares = jnp.sum(widened * widened, axis=0, keepdims=True)
        weight = 1.0 / (squares / (draws - 1) + epsilon)
        high = weight.astype(jnp.bfloat16).astype(jnp.float32)
        low = weight - high
        base = col * tokens + t * piece + j * size
        places = (base + lax.broadcasted_iota(jnp.int32, (docs, size), 1)).astype(jnp.float32)
        inside = (places >= doc_starts) & (places < doc_ends)
        member = jnp.concatenate(
            [jnp.where(inside, high, 0.0), jnp.where(inside, low, 0.0)], axis=0
        ).astype(jnp.bfloat16)

        def add_strip(n, carry):
            begin = pl.multiple_of(n * strip, strip)
            cov = jnp.dot(
                turned[pl.ds(begin, strip), :], block, preferred_element_type=jnp.float32
            )
            signed = cov * jnp.abs(cov)
            top = signed.astype(jnp.bfloat16)
            rest = (signed - top.astype(jnp.float32)).astype(jnp.bfloat16)
            dims = (((1,), (1,)), ((), ()))
            pooled = lax.dot_general(top, member, dims, preferred_element_type=jnp.float32)
            pooled += lax.dot_general(rest, member, dims, preferred_element_type=jnp.float32)
            acc[pl.ds(begin, strip), :] += pooled
            return carry

        lax.fori_loop(0, queries // strip, add_strip, 0, unroll=True)

    order = [q, partner] + columns + diagonals

    acc[...] = jnp.zeros_like(acc)
    stage(0, [], first=True)
    for k in range(1, n_m):
        down = lax.rem(m + n_m - k, n_m)
        block = whole_q.at[2 * down + c]
        remote(block, block, sq.at[down], rq.at[down], (2 * down + c, q)).wait_recv()
        copy = remote(block, block, sf.at[down], rf.at[down], (sibling, q))
        copy.start()
        started.append(copy)
    for k in range(n_m):
        block = whole_q.at[2 * k + 1 - c]
        remote(block, block, sf.at[k], rf.at[k], (sibling, q)).wait_recv()
    for copy in locals_:
        copy.wait()

    slots = jnp.broadcast_to(slots_ref[...].astype(jnp.float32), (draws, draws // per_chain))
    row = lax.broadcasted_iota(jnp.int32, slots.shape, 0)
    slot = lax.broadcasted_iota(jnp.int32, slots.shape, 1)
    offset = row - slot * per_chain
    chosen = jnp.where(
        (offset >= 0) & (offset < per_chain), slots * per_chain + offset.astype(jnp.float32), 0.0
    )
    source = jnp.sum(chosen, axis=1, keepdims=True)
    place = lax.broadcasted_iota(jnp.int32, (draws, draws), 1).astype(jnp.float32)
    moves = jnp.where(place == source, 1.0, 0.0).astype(jnp.bfloat16)
    everything = whole_q[...].reshape(draws, queries)
    for n in range(queries // strip):
        part = jnp.dot(
            moves, everything[:, n * strip:(n + 1) * strip], preferred_element_type=jnp.float32
        )
        squares = jnp.sum(part * part, axis=0, keepdims=True)
        scales[:, n * strip:(n + 1) * strip] = (
            1.0 / (squares / (draws - 1) + epsilon) / ((draws - 1) * (draws - 1))
        )
        turned[n * strip:(n + 1) * strip, :] = jnp.transpose(part).astype(jnp.bfloat16)

    def step(j, carry):
        units = [functools.partial(unit, col, j - 1) for col in order]
        units[n_a + 1] = lambda: (settle(j - 1), unit(order[n_a + 1], j - 1))
        stage(j, units)
        return carry

    lax.fori_loop(1, chunks, step, 0)
    for i in range(lag):
        pass_on(chunks - 1, ranks[n_t - lag + i])

    def last(i, carry):
        col = jnp.int32(0)
        for k in range(n_q):
            col = jnp.where(i == k, order[k], col)
        unit(col, chunks - 1)
        return carry

    lax.fori_loop(0, n_a + 1, last, 0)
    settle(chunks - 1)
    lax.fori_loop(n_a + 1, n_q, last, 0)

    for n in range(queries // strip):
        flat = jnp.transpose(acc[n * strip:(n + 1) * strip, :])
        out_ref[:, n * strip:(n + 1) * strip] = (
            (flat[0:docs] + flat[docs:2 * docs])
            * scales[:, n * strip:(n + 1) * strip]
            / (doc_ends - doc_starts)
        )

    for copy in started:
        copy.wait_send()
    for j in range(chunks):
        sent = cent.at[pl.ds(0, n_t - 1), j]
        remote(sent, sent, sa.at[j], ra.at[j, 0], (sibling, q)).wait_send()
        full = held.at[q, j]
        remote(full, full, sb.at[j], rb.at[j, 0], (t, partner)).wait_send()
        for k in range(n_a - 1):
            remote(full, full, sr.at[j, others[k]], rr.at[j, 0, 0], (t, partner)).wait_send()
            first = held.at[q, j, :, :, pl.ds(0, half)]
            remote(first, first, s0.at[j, others[k]], r0.at[j, 0], (t, partner)).wait_send()
            remote(first, first, sh.at[j, others[k]], rh.at[j, 0], (t, partner)).wait_send()


def fused(train_losses, query_losses, chain_slots, doc_lengths, n_t, n_q):
    draws_here, tokens = train_losses.shape
    queries = query_losses.shape[1]
    docs = doc_lengths.shape[0]
    draws = draws_here * n_t
    size = tokens // n_t // chunks
    width = chunks * size + queries // n_t
    n_m, n_a = n_t // 2, n_q // 2
    dma = pltpu.SemaphoreType.DMA
    bf16 = jnp.bfloat16
    vmem = pl.BlockSpec(memory_space=pltpu.VMEM)
    return pl.pallas_call(
        functools.partial(fused_kernel, n_t, n_q),
        out_shape=jax.ShapeDtypeStruct((docs, queries), jnp.float32),
        in_specs=[vmem] * 4,
        out_specs=vmem,
        scratch_shapes=[
            pltpu.VMEM((n_t, 1, width), jnp.float32),
            pltpu.VMEM((n_t, 1, width), jnp.float32),
            pltpu.VMEM((n_t, 1, width), jnp.float32),
            pltpu.VMEM((n_t, chunks, draws_here, size), bf16),
            pltpu.VMEM((draws_here, queries), bf16),
            pltpu.VMEM((n_q, chunks, n_t, draws_here, size), bf16),
            pltpu.VMEM((n_t, draws_here, queries), bf16),
            pltpu.VMEM((queries, draws), bf16),
            pltpu.VMEM((1, queries), jnp.float32),
            pltpu.VMEM((queries, 2 * docs), jnp.float32),
            dma((n_t,)), dma((n_t,)), dma((n_t,)), dma((n_t,)),
            dma((chunks,)), dma((chunks, n_t)),
            dma((n_m,)), dma((n_m,)), dma((n_m,)), dma((n_m,)),
            dma((chunks,)), dma((chunks, n_t)),
            dma((chunks, n_a)), dma((chunks, n_t, n_a)),
            dma((chunks, n_a)), dma((chunks, n_a)),
            dma((chunks, n_a)), dma((chunks, n_a)),
            dma((chunks + 1,)),
        ],
        compiler_params=pltpu.CompilerParams(
            collective_id=0, has_side_effects=True, vmem_limit_bytes=48 << 20
        ),
    )(train_losses, query_losses, chain_slots.reshape(1, -1), doc_lengths.reshape(1, -1))


def scatter_kernel(n_t, p_ref, out_ref, near, total, far, s1, r1, s2, r2):
    t = lax.axis_index("train")
    q = lax.axis_index("query")
    n_m = n_t // 2
    m, c = t // 2, lax.rem(t, 2)
    sibling = 2 * m + 1 - c
    barrier = pltpu.get_barrier_semaphore()
    pl.semaphore_signal(barrier, inc=1, device_id=(sibling, q), device_id_type=MESH)
    for k in range(1, n_m):
        other = 2 * lax.rem(m + k, n_m) + c
        pl.semaphore_signal(barrier, inc=1, device_id=(other, q), device_id_type=MESH)
    pl.semaphore_wait(barrier, n_m)
    started = []
    chips = [lax.rem(m + k, n_m) for k in range(1, n_m)] + [m]
    for chip in chips:
        copy = remote(p_ref.at[chip, 1 - c], near.at[chip], s1.at[chip], r1.at[chip], (sibling, q))
        copy.start()
        started.append(copy)
    for chip in chips:
        remote(near.at[chip], near.at[chip], s1.at[chip], r1.at[chip], (sibling, q)).wait_recv()
        total[chip] = p_ref[chip, c] + near[chip]
        if chip is not m:
            copy = remote(total.at[chip], far.at[m], s2.at[chip], r2.at[m], (2 * chip + c, q))
            copy.start()
            started.append(copy)
    result = total[m]
    for k in range(1, n_m):
        chip = lax.rem(m + n_m - k, n_m)
        remote(far.at[chip], far.at[chip], s2.at[chip], r2.at[chip], (2 * chip + c, q)).wait_recv()
        result = result + far[chip]
    out_ref[...] = result
    for copy in started:
        copy.wait_send()


def scatter(partial, n_t):
    docs, queries = partial.shape
    here = docs // n_t
    n_m = n_t // 2
    dma = pltpu.SemaphoreType.DMA
    block = pltpu.VMEM((n_m, here, queries), jnp.float32)
    return pl.pallas_call(
        functools.partial(scatter_kernel, n_t),
        out_shape=jax.ShapeDtypeStruct((here, queries), jnp.float32),
        in_specs=[pl.BlockSpec(memory_space=pltpu.VMEM)],
        out_specs=pl.BlockSpec(memory_space=pltpu.VMEM),
        scratch_shapes=[block, block, block, dma((n_m,)), dma((n_m,)), dma((n_m,)), dma((n_m,))],
        compiler_params=pltpu.CompilerParams(
            collective_id=1, has_side_effects=True, vmem_limit_bytes=16 << 20
        ),
    )(partial.reshape(n_m, 2, here, queries))


def shards(train_losses, query_losses, chain_slots, doc_lengths):
    n_t = lax.axis_size("train")
    n_q = lax.axis_size("query")
    partial = fused(train_losses, query_losses, chain_slots, doc_lengths, n_t, n_q)
    return scatter(partial, n_t)


def solution(mesh):
    in_specs = (P("train", "query"), P("train", "query"), P(), P())
    out_specs = P("train", "query")
    return jax.shard_map(shards, mesh=mesh, in_specs=in_specs, out_specs=out_specs, check_vma=False)
```

```python
import functools

import jax
import jax.numpy as jnp
from jax import lax
from jax.experimental import pallas as pl
from jax.experimental.pallas import tpu as pltpu
from jax.sharding import PartitionSpec as P

MESH = pl.DeviceIdType.MESH
epsilon = 1e-06
per_chain = 8


def remote(src, dst, send, recv, device):
    return pltpu.make_async_remote_copy(
        src_ref=src, dst_ref=dst, send_sem=send, recv_sem=recv, device_id=device, device_id_type=MESH
    )


chunks = 2
delay = 3


def fused_kernel(
    n_t, n_q, x_ref, y_ref, slots_ref, lengths_ref, out_ref,
    sums, parts, means, cent, centq, held, whole_q, turned, scales, acc,
    s1, r1, s2, r2, sa, ra, sq, rq, sf, rf, sb, rb, sr, rr, s0, r0, sh, rh, local_sem,
):
    t = lax.axis_index("train")
    q = lax.axis_index("query")
    n_m, n_a = n_t // 2, n_q // 2
    m, c = t // 2, lax.rem(t, 2)
    sibling = 2 * m + 1 - c
    a, b = q // 2, lax.rem(q, 2)
    partner = 2 * a + 1 - b
    others = [lax.rem(a + k, n_a) for k in range(1, n_a)]
    columns = [2 * other + b for other in others]
    diagonals = [2 * other + 1 - b for other in others]
    size = cent.shape[3]
    half = size // 2
    piece = chunks * size
    queries = y_ref.shape[1]
    spread = queries // n_t
    draws = x_ref.shape[0] * n_t
    tokens = x_ref.shape[1]
    docs = out_ref.shape[0]

    barrier = pltpu.get_barrier_semaphore()
    for k in range(1, n_t):
        pl.semaphore_signal(barrier, inc=1, device_id=(lax.rem(t + k, n_t), q), device_id_type=MESH)
    for target in [partner] + columns:
        pl.semaphore_signal(barrier, inc=1, device_id=(t, target), device_id_type=MESH)
    for r in range(n_t):
        sums[r, :, 0:piece] = jnp.sum(x_ref[:, r * piece:(r + 1) * piece], axis=0, keepdims=True)
        sums[r, :, piece:piece + spread] = jnp.sum(
            y_ref[:, r * spread:(r + 1) * spread], axis=0, keepdims=True
        )
    pl.semaphore_wait(barrier, n_t - 1 + n_a)

    sends, sources = [sibling], [sibling]
    for k in range(1, n_m):
        up, down = lax.rem(m + k, n_m), lax.rem(m + n_m - k, n_m)
        sends += [2 * up + c, 2 * up + 1 - c]
        sources += [2 * down + c, 2 * down + 1 - c]

    started = []
    for r in sends:
        copy = remote(sums.at[r], parts.at[t], s1.at[r], r1.at[t], (r, q))
        copy.start()
        started.append(copy)
    total = sums[t]
    for r in sources:
        remote(parts.at[r], parts.at[r], s1.at[r], r1.at[r], (r, q)).wait_recv()
        total = total + parts[r]
    means[t] = total / draws
    for r in sends:
        copy = remote(means.at[t], means.at[t], s2.at[r], r2.at[t], (r, q))
        copy.start()
        started.append(copy)

    def center(r, j):
        begin = pl.multiple_of(r * piece + j * size, 128)
        mean = means[r, :, j * size:(j + 1) * size]
        cent[r, j] = (x_ref[:, pl.ds(begin, size)] - mean).astype(jnp.bfloat16)

    def center_query(r):
        begin = pl.multiple_of(r * spread, 128)
        centq[:, pl.ds(begin, spread)] = (
            y_ref[:, pl.ds(begin, spread)] - means[r, :, piece:piece + spread]
        ).astype(jnp.bfloat16)

    def spread_block(src, j, tp):
        remote(src, held.at[q, j, tp], sb.at[j], rb.at[j, tp], (t, partner)).start()
        for k in range(n_a - 1):
            remote(
                src, held.at[q, j, tp], sr.at[j, others[k]], rr.at[j, tp, a], (t, columns[k])
            ).start()

    def pass_on(j, tp):
        block = held.at[partner, j, tp]
        remote(block, block, sb.at[j], rb.at[j, tp], (t, partner)).wait_recv()
        first = held.at[partner, j, tp, :, pl.ds(0, half)]
        for k in range(n_a - 1):
            remote(first, first, s0.at[j, others[k]], r0.at[j, a], (t, columns[k])).start()
        for k in range(n_a - 1):
            block = held.at[columns[k], j, tp]
            remote(
                block, block, sr.at[j, others[k]], rr.at[j, tp, others[k]], (t, columns[k])
            ).wait_recv()
            second = held.at[columns[k], j, tp, :, pl.ds(half, half)]
            remote(second, second, sh.at[j, others[k]], rh.at[j, others[k]], (t, partner)).start()

    locals_ = []
    for j in range(chunks):
        center(t, j)
        copy = pltpu.make_async_copy(cent.at[t, j], held.at[q, j, t], local_sem.at[j])
        copy.start()
        locals_.append(copy)
    center_query(t)
    for j in range(chunks):
        for r in sends:
            if j == 0:
                remote(means.at[r], means.at[r], s2.at[r], r2.at[r], (r, q)).wait_recv()
            center(r, j)
            remote(cent.at[r, j], held.at[q, j, t], sa.at[j], ra.at[j, t], (r, q)).start()
        if j == 0:
            spread_block(cent.at[t, 0], 0, t)
            for r in sends:
                center_query(r)
            for k in range(1, n_m):
                up = lax.rem(m + k, n_m)
                copy = remote(centq, whole_q.at[t], sq.at[up], rq.at[m], (2 * up + c, q))
                copy.start()
                started.append(copy)
            copy = remote(centq, whole_q.at[t], sf.at[m], rf.at[m], (sibling, q))
            copy.start()
            started.append(copy)
            ownq = pltpu.make_async_copy(centq, whole_q.at[t], local_sem.at[chunks])
            ownq.start()
            locals_.append(ownq)

    ranks = [t] + sources
    lag = min(delay, n_t - 1)

    def stage(j, units, first=False):
        due = 0
        for i, tp in enumerate(ranks):
            if i == 0:
                if not first:
                    spread_block(cent.at[t, j], j, t)
            else:
                block = held.at[q, j, tp]
                remote(block, block, sa.at[j], ra.at[j, tp], (tp, q)).wait_recv()
                spread_block(block, j, tp)
            if i >= lag:
                pass_on(j, ranks[i - lag])
            elif not first:
                pass_on(j - 1, ranks[n_t - lag + i])
            while due < len(units) and lag + due * (n_t - lag) // len(units) <= i + 1:
                units[due]()
                due += 1
        for unit in units[due:]:
            unit()

    def settle(j):
        for k in range(n_a - 1):
            first = held.at[diagonals[k], j, :, :, pl.ds(0, half)]
            remote(first, first, s0.at[j, others[k]], r0.at[j, others[k]], (t, columns[k])).wait_recv()
            second = held.at[diagonals[k], j, :, :, pl.ds(half, half)]
            remote(second, second, sh.at[j, others[k]], rh.at[j, others[k]], (t, partner)).wait_recv()

    wide = jnp.broadcast_to(lengths_ref[...].astype(jnp.float32), (docs, docs))
    row = lax.broadcasted_iota(jnp.int32, (docs, docs), 0)
    column = lax.broadcasted_iota(jnp.int32, (docs, docs), 1)
    doc_ends = jnp.sum(jnp.where(column <= row, wide, 0.0), axis=1, keepdims=True)
    doc_starts = jnp.sum(jnp.where(column < row, wide, 0.0), axis=1, keepdims=True)
    strip = min(512, queries)

    def unit(col, j):
        block = held[col, j].reshape(draws, size)
        widened = block.astype(jnp.float32)
        squares = jnp.sum(widened * widened, axis=0, keepdims=True)
        weight = 1.0 / (squares / (draws - 1) + epsilon)
        high = weight.astype(jnp.bfloat16).astype(jnp.float32)
        low = weight - high
        base = col * tokens + t * piece + j * size
        places = (base + lax.broadcasted_iota(jnp.int32, (docs, size), 1)).astype(jnp.float32)
        inside = (places >= doc_starts) & (places < doc_ends)
        member = jnp.concatenate(
            [jnp.where(inside, high, 0.0), jnp.where(inside, low, 0.0)], axis=0
        ).astype(jnp.bfloat16)

        def add_strip(n, carry):
            begin = pl.multiple_of(n * strip, strip)
            cov = jnp.dot(
                turned[pl.ds(begin, strip), :], block, preferred_element_type=jnp.float32
            )
            signed = cov * jnp.abs(cov)
            top = signed.astype(jnp.bfloat16)
            rest = (signed - top.astype(jnp.float32)).astype(jnp.bfloat16)
            dims = (((1,), (1,)), ((), ()))
            pooled = lax.dot_general(top, member, dims, preferred_element_type=jnp.float32)
            pooled += lax.dot_general(rest, member, dims, preferred_element_type=jnp.float32)
            acc[pl.ds(begin, strip), :] += pooled
            return carry

        lax.fori_loop(0, queries // strip, add_strip, 0, unroll=True)

    order = [q, partner] + columns + diagonals

    acc[...] = jnp.zeros_like(acc)
    stage(0, [], first=True)
    for k in range(1, n_m):
        down = lax.rem(m + n_m - k, n_m)
        block = whole_q.at[2 * down + c]
        remote(block, block, sq.at[down], rq.at[down], (2 * down + c, q)).wait_recv()
        copy = remote(block, block, sf.at[down], rf.at[down], (sibling, q))
        copy.start()
        started.append(copy)
    for k in range(n_m):
        block = whole_q.at[2 * k + 1 - c]
        remote(block, block, sf.at[k], rf.at[k], (sibling, q)).wait_recv()
    for copy in locals_:
        copy.wait()

    slots = jnp.broadcast_to(slots_ref[...].astype(jnp.float32), (draws, draws // per_chain))
    row = lax.broadcasted_iota(jnp.int32, slots.shape, 0)
    slot = lax.broadcasted_iota(jnp.int32, slots.shape, 1)
    offset = row - slot * per_chain
    chosen = jnp.where(
        (offset >= 0) & (offset < per_chain), slots * per_chain + offset.astype(jnp.float32), 0.0
    )
    source = jnp.sum(chosen, axis=1, keepdims=True)
    place = lax.broadcasted_iota(jnp.int32, (draws, draws), 1).astype(jnp.float32)
    moves = jnp.where(place == source, 1.0, 0.0).astype(jnp.bfloat16)
    everything = whole_q[...].reshape(draws, queries)
    for n in range(queries // strip):
        part = jnp.dot(
            moves, everything[:, n * strip:(n + 1) * strip], preferred_element_type=jnp.float32
        )
        squares = jnp.sum(part * part, axis=0, keepdims=True)
        scales[:, n * strip:(n + 1) * strip] = (
            1.0 / (squares / (draws - 1) + epsilon) / ((draws - 1) * (draws - 1))
        )
        turned[n * strip:(n + 1) * strip, :] = jnp.transpose(part).astype(jnp.bfloat16)

    def step(j, carry):
        units = [functools.partial(unit, col, j - 1) for col in order]
        units[n_a + 1] = lambda: (settle(j - 1), unit(order[n_a + 1], j - 1))
        stage(j, units)
        return carry

    lax.fori_loop(1, chunks, step, 0)
    for i in range(lag):
        pass_on(chunks - 1, ranks[n_t - lag + i])

    def last(i, carry):
        col = jnp.int32(0)
        for k in range(n_q):
            col = jnp.where(i == k, order[k], col)
        unit(col, chunks - 1)
        return carry

    lax.fori_loop(0, n_a + 1, last, 0)
    settle(chunks - 1)
    lax.fori_loop(n_a + 1, n_q, last, 0)

    for n in range(queries // strip):
        flat = jnp.transpose(acc[n * strip:(n + 1) * strip, :])
        out_ref[:, n * strip:(n + 1) * strip] = (
            (flat[0:docs] + flat[docs:2 * docs])
            * scales[:, n * strip:(n + 1) * strip]
            / (doc_ends - doc_starts)
        )

    for copy in started:
        copy.wait_send()
    for j in range(chunks):
        sent = cent.at[pl.ds(0, n_t - 1), j]
        remote(sent, sent, sa.at[j], ra.at[j, 0], (sibling, q)).wait_send()
        full = held.at[q, j]
        remote(full, full, sb.at[j], rb.at[j, 0], (t, partner)).wait_send()
        for k in range(n_a - 1):
            remote(full, full, sr.at[j, others[k]], rr.at[j, 0, 0], (t, partner)).wait_send()
            first = held.at[q, j, :, :, pl.ds(0, half)]
            remote(first, first, s0.at[j, others[k]], r0.at[j, 0], (t, partner)).wait_send()
            remote(first, first, sh.at[j, others[k]], rh.at[j, 0], (t, partner)).wait_send()


def fused(train_losses, query_losses, chain_slots, doc_lengths, n_t, n_q):
    draws_here, tokens = train_losses.shape
    queries = query_losses.shape[1]
    docs = doc_lengths.shape[0]
    draws = draws_here * n_t
    size = tokens // n_t // chunks
    width = chunks * size + queries // n_t
    n_m, n_a = n_t // 2, n_q // 2
    dma = pltpu.SemaphoreType.DMA
    bf16 = jnp.bfloat16
    vmem = pl.BlockSpec(memory_space=pltpu.VMEM)
    return pl.pallas_call(
        functools.partial(fused_kernel, n_t, n_q),
        out_shape=jax.ShapeDtypeStruct((docs, queries), jnp.float32),
        in_specs=[vmem] * 4,
        out_specs=vmem,
        scratch_shapes=[
            pltpu.VMEM((n_t, 1, width), jnp.float32),
            pltpu.VMEM((n_t, 1, width), jnp.float32),
            pltpu.VMEM((n_t, 1, width), jnp.float32),
            pltpu.VMEM((n_t, chunks, draws_here, size), bf16),
            pltpu.VMEM((draws_here, queries), bf16),
            pltpu.VMEM((n_q, chunks, n_t, draws_here, size), bf16),
            pltpu.VMEM((n_t, draws_here, queries), bf16),
            pltpu.VMEM((queries, draws), bf16),
            pltpu.VMEM((1, queries), jnp.float32),
            pltpu.VMEM((queries, 2 * docs), jnp.float32),
            dma((n_t,)), dma((n_t,)), dma((n_t,)), dma((n_t,)),
            dma((chunks,)), dma((chunks, n_t)),
            dma((n_m,)), dma((n_m,)), dma((n_m,)), dma((n_m,)),
            dma((chunks,)), dma((chunks, n_t)),
            dma((chunks, n_a)), dma((chunks, n_t, n_a)),
            dma((chunks, n_a)), dma((chunks, n_a)),
            dma((chunks, n_a)), dma((chunks, n_a)),
            dma((chunks + 1,)),
        ],
        compiler_params=pltpu.CompilerParams(
            collective_id=0, has_side_effects=True, vmem_limit_bytes=48 << 20
        ),
    )(train_losses, query_losses, chain_slots.reshape(1, -1), doc_lengths.reshape(1, -1))


def scatter_kernel(n_t, p_ref, out_ref, near, total, far, s1, r1, s2, r2):
    t = lax.axis_index("train")
    q = lax.axis_index("query")
    n_m = n_t // 2
    m, c = t // 2, lax.rem(t, 2)
    sibling = 2 * m + 1 - c
    barrier = pltpu.get_barrier_semaphore()
    pl.semaphore_signal(barrier, inc=1, device_id=(sibling, q), device_id_type=MESH)
    for k in range(1, n_m):
        other = 2 * lax.rem(m + k, n_m) + c
        pl.semaphore_signal(barrier, inc=1, device_id=(other, q), device_id_type=MESH)
    pl.semaphore_wait(barrier, n_m)
    started = []
    chips = [lax.rem(m + k, n_m) for k in range(1, n_m)] + [m]
    for chip in chips:
        copy = remote(p_ref.at[chip, 1 - c], near.at[chip], s1.at[chip], r1.at[chip], (sibling, q))
        copy.start()
        started.append(copy)
    for chip in chips:
        remote(near.at[chip], near.at[chip], s1.at[chip], r1.at[chip], (sibling, q)).wait_recv()
        total[chip] = p_ref[chip, c] + near[chip]
        if chip is not m:
            copy = remote(total.at[chip], far.at[m], s2.at[chip], r2.at[m], (2 * chip + c, q))
            copy.start()
            started.append(copy)
    result = total[m]
    for k in range(1, n_m):
        chip = lax.rem(m + n_m - k, n_m)
        remote(far.at[chip], far.at[chip], s2.at[chip], r2.at[chip], (2 * chip + c, q)).wait_recv()
        result = result + far[chip]
    out_ref[...] = result
    for copy in started:
        copy.wait_send()


def scatter(partial, n_t):
    docs, queries = partial.shape
    here = docs // n_t
    n_m = n_t // 2
    dma = pltpu.SemaphoreType.DMA
    block = pltpu.VMEM((n_m, here, queries), jnp.float32)
    return pl.pallas_call(
        functools.partial(scatter_kernel, n_t),
        out_shape=jax.ShapeDtypeStruct((here, queries), jnp.float32),
        in_specs=[pl.BlockSpec(memory_space=pltpu.VMEM)],
        out_specs=pl.BlockSpec(memory_space=pltpu.VMEM),
        scratch_shapes=[block, block, block, dma((n_m,)), dma((n_m,)), dma((n_m,)), dma((n_m,))],
        compiler_params=pltpu.CompilerParams(
            collective_id=1, has_side_effects=True, vmem_limit_bytes=16 << 20
        ),
    )(partial.reshape(n_m, 2, here, queries))


def shards(train_losses, query_losses, chain_slots, doc_lengths):
    n_t = lax.axis_size("train")
    n_q = lax.axis_size("query")
    partial = fused(train_losses, query_losses, chain_slots, doc_lengths, n_t, n_q)
    return scatter(partial, n_t)


def solution(mesh):
    in_specs = (P("train", "query"), P("train", "query"), P(), P())
    out_specs = P("train", "query")
    return jax.shard_map(shards, mesh=mesh, in_specs=in_specs, out_specs=out_specs, check_vma=False)
```
